256 devices in a mesh: cls: 16 (over y, x), ori: 16 (over z, core).
Axes of the slice: x: 4, y: 4, z: 8, core: 2. Of those that a mesh axis runs over, the one named last changes fastest.
Arguments:
- images: bfloat16 [1024, 2, 2048], P('ori'), may hold values from -500 to 500
- projections: bfloat16 [16, 2048, 2, 2048], P('cls', 'ori'), may hold values from -1 to 1
- ctf_table: bfloat16 [64, 2048], replicated, may hold values from 0.099609375 to 1
- ctf_index: int32 [1024], P('ori'), may hold values from 0 to 63
- centre: int32 [1024, 2], P('ori'), may hold values from -4 to 4
- ranges: int32 [1024, 4], P('ori'), may hold values from 0 to 15, as said below
- inv_noise: float32 [2048], replicated, may hold values from 0.3 to 3
Outputs:
- data_sums: float32 [16, 2048, 2, 2048], P('cls', 'ori')
- ctf_sums: float32 [16, 2048, 2048], P('cls', 'ori')
- log_evidence: float32 [1024], P('ori')
The draws below stay inside these ranges and needn't reach their ends.
Inputs may be any that keep to these rules, and one draw needn't show every extreme that they name: Each row lists 4 different ranges. Among the rows of one index of ori (aligned blocks of 64 rows) no range is listed by more than 32 rows, and one range is listed by exactly 32 rows in every block.
All inputs are finite; a program needn't handle non-finite values.
Results may differ from the reference program's by a relative error of at most 0.0065.
Values may be sent and summed in bfloat16 or wider, within the bound.
A program may use at most 128 MiB of HBM per device.

```python
import math
import jax
import jax.numpy as jnp
from jax import lax

KX = 32
KY = 64
COEFS = 2048
BOX = 256
CTF_GROUPS = 64
PRUNE = 4
TRANS = 9
ORI_DEV = 128
PART_DEV = 64
CLASSES = 16
ORIENT = 2048
PARTICLES = 1024
CAP = 32
N_ORI = 16


proj_scale = 0.0148


mean_gain = 0.644


def unit_normals(row_key):
    return jnp.clip(jax.random.normal(row_key, (2, COEFS), jnp.float32), -5.0, 5.0)


def class_gain(class_id):
    return 0.6 + 1.2 * class_id.astype(jnp.float32) / max(CLASSES - 1, 1)


def common_part(base_key, range_id):
    return unit_normals(jax.random.fold_in(jax.random.fold_in(base_key, 23), range_id))


def orient_part(base_key, class_id, orient_id):
    return unit_normals(jax.random.fold_in(jax.random.fold_in(jax.random.fold_in(base_key, 11), class_id), orient_id))


def projection_rows(base_key, class_ids, orient_ids):

    def single_row(class_id, orient_id):
        common = common_part(base_key, orient_id // ORI_DEV)
        own_rows = orient_part(base_key, class_id, orient_id)
        return proj_scale * (common + class_gain(class_id) * own_rows)
    return jax.vmap(single_row)(class_ids, orient_ids)


def route_table(base_key):
    route_key = jax.random.fold_in(base_key, 13)
    range_count = ORIENT // ORI_DEV
    hot_rank = jax.random.randint(jax.random.fold_in(route_key, 0), (), 0, range_count).astype(jnp.int32)

    def block_routes(block_id):
        block_key = jax.random.fold_in(route_key, block_id + 1)
        shuffle = jax.random.permutation(jax.random.fold_in(block_key, 0), range_count - 1).astype(jnp.int32)
        others = shuffle + (shuffle >= hot_rank).astype(jnp.int32)
        rank_order = jnp.concatenate([hot_rank[None], others])
        listing = rank_order[jnp.arange(PART_DEV * PRUNE, dtype=jnp.int32) // CAP]
        route_rows = listing.reshape(PRUNE, PART_DEV).T
        row_order = jax.random.permutation(jax.random.fold_in(block_key, 1), PART_DEV)
        return route_rows[row_order]
    blocks = lax.map(block_routes, jnp.arange(range_count, dtype=jnp.int32))
    return blocks.reshape(PARTICLES, PRUNE).astype(jnp.int32)


def centre_table(base_key):
    return jax.random.randint(jax.random.fold_in(base_key, 17), (PARTICLES, 2), -4, 5).astype(jnp.int32)


def phase_turn(rows, shifts, trans_pick):
    coef_index = jnp.arange(COEFS, dtype=jnp.int32)
    freq_x = coef_index % KX
    freq_y = coef_index // KX - KY // 2
    move_x = shifts[:, 0] + trans_pick // 3 - 1
    move_y = shifts[:, 1] + trans_pick % 3 - 1
    phase_sum = freq_x[None, :] * move_x[:, None] + freq_y[None, :] * move_y[:, None]
    angles = phase_sum.astype(jnp.float32) * (2.0 * math.pi / BOX)
    cosine = jnp.cos(angles)
    sine_part = jnp.sin(angles)
    real_part = rows[:, 0, :] * cosine - rows[:, 1, :] * sine_part
    imag_part = rows[:, 0, :] * sine_part + rows[:, 1, :] * cosine
    return jnp.stack([real_part, imag_part], axis=1)


def draw_projections(key, part):

    def class_block(class_id):
        class_rows = projection_rows(key, jnp.full((ORIENT,), class_id, jnp.int32), jnp.arange(ORIENT, dtype=jnp.int32))
        return class_rows.astype(jnp.bfloat16)
    return lax.map(class_block, jnp.arange(CLASSES, dtype=jnp.int32))


def draw_ranges(key, part):
    return route_table(key)


def draw_centre(key, part):
    return centre_table(key)


def draw_images(key, part):
    image_key = jax.random.fold_in(key, 19)
    amplitude = jnp.exp(jax.random.uniform(jax.random.fold_in(image_key, 0), (PARTICLES,), jnp.float32, math.log(0.6), math.log(1.5)))
    noise_field = jnp.clip(jax.random.normal(jax.random.fold_in(image_key, 1), (PARTICLES, 2, COEFS), jnp.float32), -6.0, 6.0)
    pictures = noise_field * amplitude[:, None, None]
    routes = route_table(key)
    shifts = centre_table(key)
    unit_cross = 2.0 * COEFS * mean_gain
    centre_pick = jnp.full((PARTICLES,), TRANS // 2, jnp.int32)
    weak_slot = jax.random.randint(jax.random.fold_in(image_key, 3), (PARTICLES,), 0, PRUNE).astype(jnp.int32)
    range_lift = jax.random.uniform(jax.random.fold_in(image_key, 4), (PARTICLES, PRUNE), jnp.float32, 3.5, 6.0)
    for slot in range(PRUNE):
        common_rows = jax.vmap(lambda range_id: common_part(key, range_id))(routes[:, slot])
        strength = jnp.where(weak_slot == slot, 0.0, range_lift[:, slot]) / (proj_scale * unit_cross)
        pictures = pictures + strength[:, None, None] * phase_turn(common_rows, shifts, centre_pick)
    slot_index = jnp.arange(PRUNE, dtype=jnp.int32)
    weak_range = jnp.sum(jnp.where(slot_index[None, :] == weak_slot[:, None], routes, 0), axis=1).astype(jnp.int32)
    spike_class = jax.random.randint(jax.random.fold_in(image_key, 5), (PARTICLES,), 0, CLASSES).astype(jnp.int32)
    spike_orient = weak_range * ORI_DEV + jax.random.randint(jax.random.fold_in(image_key, 6), (PARTICLES,), 0, ORI_DEV).astype(jnp.int32)
    spike_pick = jax.random.randint(jax.random.fold_in(image_key, 7), (PARTICLES,), 0, TRANS).astype(jnp.int32)
    own_rows = jax.vmap(lambda class_id, orient_id: orient_part(key, class_id, orient_id))(spike_class, spike_orient)
    height = math.log(CLASSES * ORI_DEV * TRANS) + jax.random.uniform(jax.random.fold_in(image_key, 8), (PARTICLES,), jnp.float32, -0.3, 1.7)
    spike_strength = height / (proj_scale * class_gain(spike_class) * unit_cross)
    pictures = pictures + spike_strength[:, None, None] * phase_turn(own_rows, shifts, spike_pick)
    return pictures.astype(jnp.bfloat16)


def set_ends(result, rng, least, high):
    extent = result.shape
    index_at = [jax.random.randint(jax.random.fold_in(rng, axis), (), 0, extent[axis]) for axis in range(len(extent))]
    result = result.at[tuple(index_at)].set(least)
    longest = extent.index(max(extent))
    index_at[longest] = (index_at[longest] + 1) % extent[longest]
    return result.at[tuple(index_at)].set(high)


def setup_inputs(seed: int = 0) -> dict:
    key_of = jax.random.split(jax.random.key(seed), 8)
    images = draw_images(jax.random.fold_in(key_of[7], 71), 0)
    projections = draw_projections(jax.random.fold_in(key_of[7], 71), 0)
    ctf_table = jnp.clip(jax.random.uniform(key_of[2], (CTF_GROUPS, COEFS), jnp.float32, 0.099609375, 1.0), 0.099609375, 1.0).astype(jnp.bfloat16)
    ctf_index = set_ends(jax.random.randint(key_of[3], (PARTICLES,), 0, CTF_GROUPS), jax.random.fold_in(key_of[3], 1), 0, CTF_GROUPS - 1).astype(jnp.int32)
    centre = draw_centre(jax.random.fold_in(key_of[7], 71), 0)
    ranges = draw_ranges(jax.random.fold_in(key_of[7], 71), 0)
    inv_noise = jnp.clip(jnp.exp(jax.random.uniform(key_of[6], (COEFS,), jnp.float32, math.log(0.3), math.log(3.0))), 0.3, 3.0)
    return {"images": images, "projections": projections, "ctf_table": ctf_table, "ctf_index": ctf_index, "centre": centre, "ranges": ranges, "inv_noise": inv_noise}


def reference(images, projections, ctf_table, ctf_index, centre, ranges, inv_noise):
    slot_count = N_ORI * CAP
    coef_index = jnp.arange(COEFS, dtype=jnp.int32)
    freq_x = coef_index % KX
    freq_y = coef_index // KX - KY // 2
    trans_index = jnp.arange(TRANS, dtype=jnp.int32)
    step_x = trans_index // 3 - 1
    step_y = trans_index % 3 - 1
    ctf_all = ctf_table[ctf_index].astype(jnp.float32)
    radians = 2.0 * math.pi / BOX
    weight_scale = CLASSES * PRUNE * ORI_DEV

    def slot_list(rank_id):
        member = jnp.any(ranges == rank_id, axis=1)
        slot_ids = jnp.argsort(jnp.where(member, 0, 1), stable=True)[:slot_count].astype(jnp.int32)
        return slot_ids, member[slot_ids]

    def shifted(slot_ids):
        pixels = images[slot_ids].astype(jnp.float32)
        ctf_curve = ctf_all[slot_ids]
        move_x = centre[slot_ids, 0][:, None] + step_x[None, :]
        move_y = centre[slot_ids, 1][:, None] + step_y[None, :]
        phase_sum = freq_x[None, None, :] * move_x[:, :, None] + freq_y[None, None, :] * move_y[:, :, None]
        angles = phase_sum.astype(jnp.float32) * radians
        cosine = jnp.cos(angles)
        sine_part = jnp.sin(angles)
        factor = (ctf_curve * inv_noise[None, :])[:, None, :]
        real_part = factor * (pixels[:, None, 0, :] * cosine + pixels[:, None, 1, :] * sine_part)
        imag_part = factor * (pixels[:, None, 1, :] * cosine - pixels[:, None, 0, :] * sine_part)
        rotated = jnp.stack([real_part, imag_part], axis=2).astype(jnp.bfloat16)
        ctf_weight = (inv_noise[None, :] * ctf_curve * ctf_curve).astype(jnp.bfloat16)
        return rotated.reshape(slot_count * TRANS, 2 * COEFS), ctf_weight

    def range_planes(rank_id):
        planes = lax.dynamic_slice_in_dim(projections, (rank_id * ORI_DEV).astype(jnp.int32), ORI_DEV, axis=1)
        flat_plane = planes.reshape(CLASSES * ORI_DEV, 2 * COEFS)
        wide_plane = planes.astype(jnp.float32)
        power_plane = (wide_plane[:, :, 0, :] * wide_plane[:, :, 0, :] + wide_plane[:, :, 1, :] * wide_plane[:, :, 1, :]).astype(jnp.bfloat16)
        return flat_plane, power_plane.reshape(CLASSES * ORI_DEV, COEFS)

    def first_pass(rank_id):
        slot_ids, is_valid = slot_list(rank_id)
        rotated, ctf_weight = shifted(slot_ids)
        flat_plane, power_plane = range_planes(rank_id)
        cross_term = jnp.dot(rotated, flat_plane.T, preferred_element_type=jnp.float32).reshape(slot_count, TRANS, CLASSES * ORI_DEV)
        energy = 0.5 * jnp.dot(ctf_weight, power_plane.T, preferred_element_type=jnp.float32)
        scores = cross_term - energy[:, None, :]
        live_scores = jnp.where(is_valid[:, None, None], scores, -1e30)
        slot_peak = jnp.max(live_scores, axis=(1, 2))
        slot_mass = jnp.where(is_valid, jnp.sum(jnp.exp(live_scores - slot_peak[:, None, None]), axis=(1, 2)), 0.0)
        return slot_ids, is_valid, scores, slot_peak, slot_mass

    slot_ids, is_valid, scores, slot_peak, slot_mass = lax.map(first_pass, jnp.arange(N_ORI, dtype=jnp.int32))
    flat_ids = slot_ids.reshape(-1)
    flat_peak = jnp.where(is_valid, slot_peak, -1e30).reshape(-1)
    peak_all = jnp.full((PARTICLES,), -1e30, jnp.float32).at[flat_ids].max(flat_peak)
    total_all = jnp.zeros((PARTICLES,), jnp.float32).at[flat_ids].add(slot_mass.reshape(-1) * jnp.exp(flat_peak - peak_all[flat_ids]))
    log_evidence = peak_all + jnp.log(total_all)

    def second_pass(packed):
        slot_ids, is_valid, scores = packed
        rotated, ctf_weight = shifted(slot_ids)
        weight = weight_scale * jnp.exp(scores - log_evidence[slot_ids][:, None, None])
        weight = jnp.where(is_valid[:, None, None], weight, 0.0)
        rounded = weight.astype(jnp.bfloat16).reshape(slot_count * TRANS, CLASSES * ORI_DEV)
        data_part = jnp.dot(rounded.T, rotated, preferred_element_type=jnp.float32)
        totals = jnp.sum(weight, axis=1).astype(jnp.bfloat16)
        ctf_part = jnp.dot(totals.T, ctf_weight, preferred_element_type=jnp.float32)
        return data_part, ctf_part

    data_parts, ctf_parts = lax.map(second_pass, (slot_ids, is_valid, scores))
    data_sums = data_parts.reshape(N_ORI, CLASSES, ORI_DEV, 2, COEFS).transpose(1, 0, 2, 3, 4).reshape(CLASSES, ORIENT, 2, COEFS)
    ctf_sums = ctf_parts.reshape(N_ORI, CLASSES, ORI_DEV, COEFS).transpose(1, 0, 2, 3).reshape(CLASSES, ORIENT, COEFS)
    return data_sums, ctf_sums, log_evidence
```

```python
import functools
import math

import jax
import jax.numpy as jnp
import numpy as np
from jax import lax
from jax.experimental import pallas as pl
from jax.experimental.pallas import tpu as pltpu
from jax.sharding import PartitionSpec as P

KX = 32
KY = 64
BOX = 256
TRANS = 9
N_CLS = 16
N_ORI = 16
SIDE = 4
PART = 64
CAP = 32
SLOTS = N_ORI * CAP
ORI_DEV = 128
COEFS = 2048
GROUPS = 64
CHUNK = COEFS // N_CLS
PRUNE = 4
RADIANS = 2.0 * math.pi / BOX
MESH = pl.DeviceIdType.MESH
F32 = jnp.float32
BF16 = jnp.bfloat16
VMEM_LIMIT = 56 * 1024 * 1024


def step_tables():
    k = np.arange(COEFS)
    kx = k % KX
    ky = k // KX - KY // 2
    cosine = np.zeros((16, COEFS), np.float32)
    sine = np.zeros((16, COEFS), np.float32)
    for a in range(TRANS):
        turn = (kx * (a // 3 - 1) + ky * (a % 3 - 1)) * RADIANS
        cosine[a] = np.cos(turn)
        sine[a] = np.sin(turn)
    return cosine, sine


def wrap(value, size):
    return lax.rem(value + size, size)


def nt_dot(left, right):
    return lax.dot_general(left, right, (((1,), (1,)), ((), ())), preferred_element_type=F32)


def tn_dot(left, right):
    return lax.dot_general(left, right, (((0,), (0,)), ((), ())), preferred_element_type=F32)


def slot_row(rows_ref, n):
    groups = []
    for q in range(4):
        parts = [rows_ref[4 * q + m, n:n + 1, :] for m in range(4)]
        groups.append((parts[0] + parts[1]) + (parts[2] + parts[3]))
    return jnp.concatenate(groups, axis=1)


def iota(shape, axis):
    return lax.broadcasted_iota(jnp.int32, shape, axis)


HALF = SLOTS // 2
COMBOS = 96
PIECE = HALF // 2


def expect_kernel(images_ref, proj_ref, ctf_ref, index_ref, centre_ref, ranges_ref, inv_ref, cos_ref, sin_ref,
                  yout_ref, w_ref, t_ref, cw_ref, log_ref,
                  ximg, pbuf, send, meta, metain, ys, pd, s_ref, joint, shared, maps, yc, hot, trig, buf_a, buf_b,
                  local_sem, z_send, z_recv, m_send, m_recv, f_send, p_send, g_recv, e_send, e_recv):
    c = lax.axis_index("cls")
    h = lax.axis_index("ori")
    x = lax.rem(c, SIDE)
    y = lax.div(c, SIDE)

    def at(dx, dy):
        return wrap(y + dy, SIDE) * SIDE + wrap(x + dx, SIDE)

    def rel(half, du, dv):
        if isinstance(half, int):
            return at(du, dv) if half == 0 else at(dv, du)
        return at(du + half * (dv - du), dv + half * (du - dv))

    barrier = pltpu.get_barrier_semaphore()

    def quad_peer(stage, j):
        if stage == 0:
            return at(j, 0), h
        if stage == 1:
            return at(0, j), h
        if stage == 2:
            return c, lax.div(h, 4) * 4 + lax.rem(h + j, 4)
        return c, lax.rem(h + 4 * j, N_ORI)

    def greet(step, carry):
        pl.semaphore_signal(barrier, inc=1, device_id=(c, wrap(h + step, N_ORI)), device_id_type=MESH)
        return carry

    for stage in (0, 1):
        for j in (1, 2, 3):
            pl.semaphore_signal(barrier, inc=1, device_id=quad_peer(stage, j), device_id_type=MESH)
    lax.fori_loop(1, N_ORI, greet, 0)
    lanes = pl.ds(pl.multiple_of(c * CHUNK, CHUNK), CHUNK)
    get_image = pltpu.make_async_copy(images_ref.at[:, :, lanes], ximg, local_sem.at[0])
    get_image.start()
    get_proj = pltpu.make_async_copy(proj_ref.at[0], pbuf, local_sem.at[1])
    get_proj.start()

    index_row = index_ref[...].astype(F32)
    member_t = jnp.zeros((N_ORI, PART), F32)
    rank = iota((N_ORI, PART), 0)
    for j in range(PRUNE):
        member_t = member_t + (ranges_ref[j:j + 1, :] == rank).astype(F32)
    above = (iota((PART, PART), 0) < iota((PART, PART), 1)).astype(BF16)
    before_t = jnp.dot(member_t.astype(BF16), above, preferred_element_type=F32)
    pos_t = before_t - 1000.0 * (1.0 - member_t)
    odd = lax.rem(h, 2).astype(F32)
    key = (before_t + 1.0) * member_t
    keys = jnp.concatenate([key * (1.0 - odd), key * odd], axis=1)
    seat = iota((CAP, PART), 0).astype(F32)
    chosen = jnp.concatenate(
        [(pos_t[r:r + 1, :] == seat).astype(BF16) for r in range(N_ORI)], axis=0
    )
    offset = (CAP * lax.rem(h, 4)).astype(F32)
    wide_seat = iota((128, PART), 0).astype(F32) - offset
    moves = centre_ref[...].astype(F32)
    combo = (moves[0:1, :] + 4.0) * 9.0 + moves[1:2, :] + 4.0
    label = jnp.concatenate([index_row + 1.0, combo, jnp.zeros((6, PART), F32)], axis=0).astype(BF16)
    for r in range(N_ORI):
        wide = (pos_t[r:r + 1, :] == wide_seat).astype(BF16)
        seated = nt_dot(label, wide)
        meta[r] = jnp.concatenate([seated[0:1, :], keys[r:r + 1, :], seated[1:3, :]], axis=0)
    get_image.wait()
    pixels = ximg[...].astype(F32)
    x0 = pixels[:, 0, :]
    x1 = pixels[:, 1, :]
    centred = jnp.concatenate([x0, x1], axis=1).astype(BF16)
    send[...] = jnp.dot(chosen, centred, preferred_element_type=F32).astype(BF16).reshape(N_ORI, CAP, 2 * CHUNK)

    pl.semaphore_wait(barrier, N_ORI - 1 + 6)

    def block_cols(block):
        return pl.ds(pl.multiple_of(block * 2 * CHUNK, 2 * CHUNK), 2 * CHUNK)

    def seat_rows(block):
        return pl.ds(pl.multiple_of(block * CAP, CAP), CAP)

    def parcel(peer, step):
        return pltpu.make_async_remote_copy(
            src_ref=send.at[peer], dst_ref=ys.at[seat_rows(h), block_cols(c)], send_sem=z_send.at[step],
            recv_sem=z_recv.at[h], device_id=(c, peer), device_id_type=MESH)

    def note(peer, step):
        return pltpu.make_async_remote_copy(
            src_ref=meta.at[peer], dst_ref=metain.at[h], send_sem=m_send.at[step],
            recv_sem=m_recv.at[h], device_id=(c, peer), device_id_type=MESH)

    def send_out(step, carry):
        peer = wrap(h + step, N_ORI)
        note(peer, step).start()
        parcel(peer, step).start()
        return carry

    lax.fori_loop(1, N_ORI, send_out, 0)
    own_rows = pltpu.make_async_copy(send.at[h], ys.at[seat_rows(h), block_cols(c)], local_sem.at[2])
    own_rows.start()
    metain[h] = meta[h]

    get_proj.wait()
    s_ref[0:ORI_DEV, 0:GROUPS] = jnp.zeros((ORI_DEV, GROUPS), F32)

    def turn_chunk(j, carry):
        cols = pl.ds(pl.multiple_of(j * CHUNK, CHUNK), CHUNK)
        both = pbuf[:, :, cols].astype(F32)
        p0 = both[:, 0, :]
        p1 = both[:, 1, :]
        power = (p0 * p0 + p1 * p1).astype(BF16)
        table = ctf_ref[:, cols].astype(F32)
        cw = (inv_ref[:, cols] * table * table).astype(BF16)
        cw_ref[:, cols] = cw
        s_ref[0:ORI_DEV, 0:GROUPS] += nt_dot(power, cw)
        for d in range(TRANS):
            rows = pl.ds(d * ORI_DEV, ORI_DEV)
            cd = cos_ref[d:d + 1, cols]
            sd = sin_ref[d:d + 1, cols]
            turned = (p0 * cd - p1 * sd, p1 * cd + p0 * sd)
            for n in (0, 1):
                coarse = turned[n].astype(BF16)
                pd[j, rows, n * CHUNK:(n + 1) * CHUNK] = coarse
                pd[j, rows, (2 + n) * CHUNK:(3 + n) * CHUNK] = (turned[n] - coarse.astype(F32)).astype(BF16)
        k = j * CHUNK + iota((1, CHUNK), 1)
        kx = lax.rem(k, KX)
        ky = lax.div(k, KX) - KY // 2
        which = iota((COMBOS, 1), 0)
        angles = (kx * (lax.div(which, 9) - 4) + ky * (lax.rem(which, 9) - 4)).astype(F32) * RADIANS
        for n, wave in ((0, jnp.cos(angles)), (1, jnp.sin(angles))):
            coarse = wave.astype(BF16)
            span = slice(n * CHUNK, (n + 1) * CHUNK)
            trig[j, 0:GROUPS, span] = jnp.zeros((GROUPS, CHUNK), BF16)
            trig[j, GROUPS:GROUPS + COMBOS, span] = coarse
            trig[j, GROUPS + COMBOS:256, span] = (wave - coarse.astype(F32)).astype(BF16)
        trig[j, 0:GROUPS, 2 * CHUNK:3 * CHUNK] = ctf_ref[:, cols]
        trig[j, GROUPS:256, 2 * CHUNK:3 * CHUNK] = jnp.zeros((2 * COMBOS, CHUNK), BF16)
        return carry

    lax.fori_loop(0, N_CLS, turn_chunk, 0)

    def arrive(step, carry):
        peer = wrap(h - step, N_ORI)
        pltpu.make_async_remote_copy(
            src_ref=send.at[h], dst_ref=ys.at[seat_rows(peer), block_cols(c)], send_sem=z_send.at[0],
            recv_sem=z_recv.at[peer], device_id=(c, peer), device_id_type=MESH).wait_recv()
        pltpu.make_async_remote_copy(
            src_ref=meta.at[h], dst_ref=metain.at[peer], send_sem=m_send.at[0],
            recv_sem=m_recv.at[peer], device_id=(c, peer), device_id_type=MESH).wait_recv()
        return carry

    own_rows.wait()
    lax.fori_loop(1, N_ORI, arrive, 0)

    def full_view(half, block):
        return ys.at[pl.ds(pl.multiple_of(half * HALF, HALF), HALF), block_cols(block)]

    def piece_view(half, block, piece):
        return ys.at[pl.ds(pl.multiple_of(half * HALF + piece * PIECE, PIECE), PIECE), block_cols(block)]

    def full_copy(half, block, target, slot):
        return pltpu.make_async_remote_copy(
            src_ref=full_view(half, block), dst_ref=full_view(half, block), send_sem=f_send.at[slot],
            recv_sem=g_recv.at[half, block, 0], device_id=(target, h), device_id_type=MESH)

    def piece_copy(half, block, piece, target, slot):
        return pltpu.make_async_remote_copy(
            src_ref=piece_view(half, block, piece), dst_ref=piece_view(half, block, piece),
            send_sem=p_send.at[slot], recv_sem=g_recv.at[half, block, piece],
            device_id=(target, h), device_id_type=MESH)

    def second_sends(half, du, t):
        for n, sign in enumerate((1, -1)):
            full_copy(half, rel(half, du, 0), rel(half, 0, sign), 4 + 4 * t + 2 * half + n).start()

    for half in (0, 1):
        for n, sign in enumerate((1, -1)):
            full_copy(half, rel(half, 0, 0), rel(half, sign, 0), 2 * half + n).start()
    for half in (0, 1):
        second_sends(half, 0, 0)

    row = slot_row(metain, 0) - 1.0
    slot_pick = (iota((GROUPS, SLOTS), 0).astype(F32) == row).astype(BF16)
    combo_pick = (iota((COMBOS, SLOTS), 0).astype(F32) == slot_row(metain, 2)).astype(BF16)
    eye = (iota((256, 256), 0) == iota((256, 256), 1)).astype(BF16)
    hot[...] = tn_dot(jnp.concatenate([slot_pick, combo_pick, combo_pick], axis=0), eye).astype(BF16)
    rest = s_ref[0:ORI_DEV, 0:GROUPS]
    energy = jnp.zeros((ORI_DEV, SLOTS), F32)
    for _ in range(3):
        part = rest.astype(BF16)
        rest = rest - part.astype(F32)
        energy = energy + jnp.dot(part, slot_pick, preferred_element_type=F32)
    less = -0.5 * energy - jnp.where(row < 0.0, 1e30, 0.0)
    for d in range(TRANS):
        s_ref[pl.ds(d * ORI_DEV, ORI_DEV), :] = less

    tall = iota((128, 128), 0).astype(F32)
    side = lax.div(iota((1, 128), 1), PART)
    listed = []
    for p in range(N_ORI // 2):
        keyed = metain[2 * p, 1:2, :] + metain[2 * p + 1, 1:2, :]
        listed.append(keyed)
        target = keyed - 1.0 + (CAP * (2 * (p % 2) + side)).astype(F32)
        target = jnp.where(keyed > 0.0, target, -1000.0)
        maps[p // 2, :, 128 * (p % 2):128 * (p % 2) + 128] = (tall == target).astype(BF16)

    def centre_rows(half, block, buf):
        rows = slice(half * HALF, half * HALF + HALF)
        freqs = pl.ds(pl.multiple_of(block * CHUNK, CHUNK), CHUNK)
        wave = jnp.dot(hot[rows, :], trig[block], preferred_element_type=F32)
        cs = wave[:, 0:CHUNK]
        sn = wave[:, CHUNK:2 * CHUNK]
        factor = wave[:, 2 * CHUNK:3 * CHUNK] * inv_ref[:, freqs]
        raw = ys[rows, block_cols(block)].astype(F32)
        x0 = raw[:, 0:CHUNK]
        x1 = raw[:, CHUNK:2 * CHUNK]
        value = jnp.concatenate([factor * (x0 * cs + x1 * sn), factor * (x1 * cs - x0 * sn)], axis=1)
        coarse = value.astype(BF16)
        buf[:, 0:2 * CHUNK] = coarse
        buf[:, 2 * CHUNK:4 * CHUNK] = (value - coarse.astype(F32)).astype(BF16)
        yc[rows, block_cols(block)] = coarse

    def add_scores(half, block, buf):
        first = pd[block, :, 0:2 * CHUNK]
        second = pd[block, :, 2 * CHUNK:4 * CHUNK]
        coarse = buf[:, 0:2 * CHUNK]
        fine = buf[:, 2 * CHUNK:4 * CHUNK]
        s_ref[:, half * HALF:half * HALF + HALF] += nt_dot(first, coarse) + (
            nt_dot(first, fine) + nt_dot(second, coarse)
        )

    def pair(before, du, dv):
        block = rel(0, du, dv)
        add_scores(1, before, buf_b)
        centre_rows(0, block, buf_a)
        block_b = rel(1, du, dv)
        add_scores(0, block, buf_a)
        centre_rows(1, block_b, buf_b)
        return block_b

    centre_rows(0, c, buf_a)
    add_scores(0, c, buf_a)
    centre_rows(1, c, buf_b)
    before = c
    for t, du, piece, onward in ((1, -1, 0, 1), (2, 1, 1, -1)):
        for half in (0, 1):
            full_copy(half, rel(half, du, 0), c, 0).wait_recv()
            piece_copy(half, rel(half, du, 0), piece, rel(half, onward, 0), 2 * half + piece).start()
        for half in (0, 1):
            second_sends(half, du, t)

    before = lax.fori_loop(0, 2, lambda n, block: pair(block, 2 * n - 1, 0), before)
    for half in (0, 1):
        for piece in (0, 1):
            piece_copy(half, rel(half, 2, 0), piece, c, 0).wait_recv()
        second_sends(half, 2, 3)

    before = pair(before, 2, 0)

    def gray(t):
        return t + lax.div(t, 2) * (1 - 2 * lax.rem(t, 2))

    def cross(t, carry):
        du = gray(t)
        for dv, piece, onward in ((-1, 0, 1), (1, 1, -1)):
            for half in (0, 1):
                full_copy(half, rel(half, du, dv), c, 0).wait_recv()
                piece_copy(half, rel(half, du, dv), piece, rel(half, 0, onward), 4 + 4 * t + 2 * half + piece).start()

        return lax.fori_loop(0, 2, lambda n, block: pair(block, du, 2 * n - 1), carry)

    before = lax.fori_loop(0, 4, cross, before)

    def corner(n, carry):
        du = gray(n)
        for half in (0, 1):
            for piece in (0, 1):
                piece_copy(half, rel(half, du, 2), piece, c, 0).wait_recv()
        return pair(carry, du, 2)

    before = lax.fori_loop(0, 4, corner, before)
    add_scores(1, before, buf_b)
    save = pltpu.make_async_copy(yc, yout_ref, local_sem.at[3])
    save.start()

    peak = s_ref[0:ORI_DEV, :]
    for d in range(1, TRANS):
        peak = jnp.maximum(peak, s_ref[pl.ds(d * ORI_DEV, ORI_DEV), :])
    peak = jnp.max(peak, axis=0, keepdims=True)
    mass = jnp.zeros((ORI_DEV, SLOTS), F32)
    for d in range(TRANS):
        rows = pl.ds(d * ORI_DEV, ORI_DEV)
        value = jnp.exp(s_ref[rows, :] - peak)
        s_ref[rows, :] = value
        mass = mass + value
    total = jnp.sum(mass, axis=0, keepdims=True)
    def split(value):
        parts = []
        for _ in range(3):
            part = value.astype(BF16).astype(F32)
            parts.append(part)
            value = value - part
        return parts

    blank = jnp.zeros((2, 128), F32)
    for q in range(4):
        span = slice(128 * q, 128 * q + 128)
        rows = jnp.concatenate(split(peak[:, span]) + split(total[:, span]) + [blank], axis=0).astype(BF16)
        spread = jnp.dot(rows, maps[q], preferred_element_type=F32)
        particle_peak = spread[0:1, :] + spread[1:2, :] + spread[2:3, :]
        particle_mass = spread[3:4, :] + spread[4:5, :] + spread[5:6, :]
        for n in (0, 1):
            half_span = slice(128 * n, 128 * n + 128)
            p = 2 * q + n
            joint[0, 0, p:p + 1, :] = jnp.where(listed[p] > 0.0, particle_peak[:, half_span], -3e38)
            joint[0, 1, p:p + 1, :] = particle_mass[:, half_span]

    def share(stage, j):
        return pltpu.make_async_remote_copy(
            src_ref=joint.at[stage], dst_ref=shared.at[stage, j - 1], send_sem=e_send.at[stage, j],
            recv_sem=e_recv.at[stage, j], device_id=quad_peer(stage, j), device_id_type=MESH)

    for stage in range(4):
        for j in (1, 2, 3):
            share(stage, j).start()
        for j in (1, 2, 3):
            share(stage, j).wait_recv()
        high = joint[stage, 0]
        for j in range(3):
            high = jnp.maximum(high, shared[stage, j, 0])
        heaps = [joint[stage, 1] * jnp.exp(joint[stage, 0] - high)]
        for j in range(3):
            heaps.append(shared[stage, j, 1] * jnp.exp(shared[stage, j, 0] - high))
        heap = (heaps[0] + heaps[2]) + (heaps[1] + heaps[3])
        if stage < 3:
            joint[stage + 1, 0] = high
            joint[stage + 1, 1] = heap
    log_all = high + jnp.log(heap)
    joint[4, 0] = log_all
    home_row = joint[4, 0, pl.ds(lax.div(h, 2), 1), :]
    log_ref[...] = jnp.where(lax.rem(h, 2) == 0, home_row[:, 0:PART], home_row[:, PART:2 * PART])
    groups = []
    for q in range(4):
        pair = jnp.concatenate([log_all[2 * q:2 * q + 1, :], log_all[2 * q + 1:2 * q + 2, :]], axis=1)
        rows = jnp.concatenate(split(pair) + [jnp.zeros((5, 256), F32)], axis=0).astype(BF16)
        back_row = nt_dot(rows, maps[q])
        groups.append(back_row[0:1, :] + back_row[1:2, :] + back_row[2:3, :])
    slot_log = jnp.concatenate(groups, axis=1)
    scale = float(N_CLS * PRUNE * ORI_DEV)
    level = jnp.where(row < 0.0, 0.0, scale * jnp.exp(peak - slot_log))
    for d in range(TRANS):
        rows = pl.ds(d * ORI_DEV, ORI_DEV)
        w_ref[rows, :] = (s_ref[rows, :] * level).astype(BF16)
    grouped = nt_dot((mass * level).astype(BF16), slot_pick)
    high = grouped.astype(BF16)
    t_ref[:, 0:GROUPS] = high
    t_ref[:, GROUPS:2 * GROUPS] = (grouped - high.astype(F32)).astype(BF16)

    def drain(step, carry):
        peer = wrap(h + step, N_ORI)
        parcel(peer, step).wait_send()
        note(peer, step).wait_send()
        return carry

    lax.fori_loop(1, N_ORI, drain, 0)

    def drain_blocks(slot, carry):
        full_copy(0, c, c, slot).wait_send()
        piece_copy(0, c, 0, c, slot).wait_send()
        return carry

    lax.fori_loop(0, 20, drain_blocks, 0)
    for stage in range(4):
        for j in (1, 2, 3):
            share(stage, j).wait_send()
    save.wait()


def expect(images, projections, ctf_table, index_row, centre, ranges, inv_row, cosine, sine):
    vmem = pl.BlockSpec(memory_space=pltpu.VMEM)
    hbm = pl.BlockSpec(memory_space=pl.ANY)
    rows = TRANS * ORI_DEV
    dma = pltpu.SemaphoreType.DMA
    return pl.pallas_call(
        expect_kernel,
        out_shape=(
            jax.ShapeDtypeStruct((SLOTS, 2 * COEFS), BF16),
            jax.ShapeDtypeStruct((rows, SLOTS), BF16),
            jax.ShapeDtypeStruct((ORI_DEV, 2 * GROUPS), BF16),
            jax.ShapeDtypeStruct((GROUPS, COEFS), BF16),
            jax.ShapeDtypeStruct((1, PART), F32),
        ),
        in_specs=[hbm, hbm] + [vmem] * 7,
        out_specs=(hbm, vmem, vmem, vmem, vmem),
        scratch_shapes=[
            pltpu.VMEM((PART, 2, CHUNK), BF16),
            pltpu.VMEM((ORI_DEV, 2, COEFS), BF16),
            pltpu.VMEM((N_ORI, CAP, 2 * CHUNK), BF16),
            pltpu.VMEM((N_ORI, 4, 128), F32),
            pltpu.VMEM((N_ORI, 4, 128), F32),
            pltpu.VMEM((SLOTS, 2 * COEFS), BF16),
            pltpu.VMEM((N_CLS, rows, 4 * CHUNK), BF16),
            pltpu.VMEM((rows, SLOTS), F32),
            pltpu.VMEM((5, 2, N_ORI // 2, 128), F32),
            pltpu.VMEM((4, 3, 2, N_ORI // 2, 128), F32),
            pltpu.VMEM((4, 128, 256), BF16),
            pltpu.VMEM((SLOTS, 2 * COEFS), BF16),
            pltpu.VMEM((SLOTS, 256), BF16),
            pltpu.VMEM((N_CLS, 256, 3 * CHUNK), BF16),
            pltpu.VMEM((HALF, 4 * CHUNK), BF16),
            pltpu.VMEM((HALF, 4 * CHUNK), BF16),
            dma((4,)),
            dma((N_ORI,)),
            dma((N_ORI,)),
            dma((N_ORI,)),
            dma((N_ORI,)),
            dma((20,)),
            dma((20,)),
            dma((2, N_CLS, 2)),
            dma((4, 4)),
            dma((4, 4)),
        ],
        compiler_params=pltpu.CompilerParams(
            collective_id=0, has_side_effects=True, vmem_limit_bytes=VMEM_LIMIT
        ),
        name="expect",
    )(images, projections, ctf_table, index_row, centre, ranges, inv_row, cosine, sine)


WIDE = 4


def back_kernel(w_ref, t_ref, y_ref, cw_ref, cos_ref, sin_ref, data_ref, ctf_ref, d_ref):
    cw = cw_ref[...]
    ctf_ref[0] = jnp.dot(t_ref[...], jnp.concatenate([cw, cw], axis=0), preferred_element_type=F32)
    d_ref[...] = jnp.dot(w_ref[...], y_ref[...], preferred_element_type=F32)

    def turn(minus, zero, plus, cd, sd):
        real = zero[0] + cd * (plus[0] + minus[0]) + sd * (plus[1] - minus[1])
        imag = zero[1] + cd * (plus[1] + minus[1]) - sd * (plus[0] - minus[0])
        return real, imag

    for part in range(WIDE):
        base = part * 2 * CHUNK
        cols = slice(part * CHUNK, part * CHUNK + CHUNK)
        for block in range(ORI_DEV // 16):
            outer = []
            for dx in range(3):
                inner = []
                for dy in range(3):
                    rows = pl.ds((dx * 3 + dy) * ORI_DEV + block * 16, 16)
                    inner.append((d_ref[rows, base:base + CHUNK], d_ref[rows, base + CHUNK:base + 2 * CHUNK]))
                outer.append(turn(*inner, cos_ref[5:6, cols], sin_ref[5:6, cols]))
            real, imag = turn(*outer, cos_ref[7:8, cols], sin_ref[7:8, cols])
            data_ref[0, block * 16:(block + 1) * 16, 0, cols] = real
            data_ref[0, block * 16:(block + 1) * 16, 1, cols] = imag


def back(w, t, ys, cw, cosine, sine):
    full = lambda *shape: pl.BlockSpec(shape, lambda j: (0,) * len(shape))
    return pl.pallas_call(
        back_kernel,
        out_shape=(
            jax.ShapeDtypeStruct((1, ORI_DEV, 2, COEFS), F32),
            jax.ShapeDtypeStruct((1, ORI_DEV, COEFS), F32),
        ),
        grid=(N_CLS // WIDE,),
        in_specs=[
            full(TRANS * ORI_DEV, SLOTS),
            full(ORI_DEV, 2 * GROUPS),
            pl.BlockSpec((SLOTS, WIDE * 2 * CHUNK), lambda j: (0, j)),
            pl.BlockSpec((GROUPS, WIDE * CHUNK), lambda j: (0, j)),
            pl.BlockSpec((16, WIDE * CHUNK), lambda j: (0, j)),
            pl.BlockSpec((16, WIDE * CHUNK), lambda j: (0, j)),
        ],
        out_specs=(
            pl.BlockSpec((1, ORI_DEV, 2, WIDE * CHUNK), lambda j: (0, 0, 0, j)),
            pl.BlockSpec((1, ORI_DEV, WIDE * CHUNK), lambda j: (0, 0, j)),
        ),
        scratch_shapes=[pltpu.VMEM((TRANS * ORI_DEV, WIDE * 2 * CHUNK), F32)],
        compiler_params=pltpu.CompilerParams(vmem_limit_bytes=VMEM_LIMIT),
        name="back",
    )(w, t, ys, cw, cosine, sine)


def shards(images, projections, ctf_table, ctf_index, centre, ranges, inv_noise):
    cosine, sine = (jnp.asarray(table) for table in step_tables())
    ys, w, t, cw, log_row = expect(
        images, projections, ctf_table, ctf_index.reshape(1, PART), centre.T, ranges.T,
        inv_noise.reshape(1, COEFS), cosine, sine,
    )
    data, ctf = back(w, t, ys, cw, cosine, sine)
    return data, ctf, log_row.reshape(PART)


def solution(mesh):
    placed = (
        P("ori", None, None),
        P("cls", "ori", None, None),
        P(),
        P("ori"),
        P("ori", None),
        P("ori", None),
        P(),
    )
    return jax.shard_map(
        shards,
        mesh=mesh,
        in_specs=placed,
        out_specs=(P("cls", "ori", None, None), P("cls", "ori", None), P("ori")),
        check_vma=False,
    )
```

```python
import functools
import math

import jax
import jax.numpy as jnp
import ml_dtypes
import numpy as np
from jax import lax
from jax.experimental import pallas as pl
from jax.experimental.pallas import tpu as pltpu
from jax.sharding import PartitionSpec as P

KX = 32
KY = 64
BOX = 256
TRANS = 9
N_CLS = 16
N_ORI = 16
SIDE = 4
PART = 64
CAP = 32
SLOTS = N_ORI * CAP
ORI_DEV = 128
COEFS = 2048
GROUPS = 64
CHUNK = COEFS // N_CLS
PRUNE = 4
RADIANS = 2.0 * math.pi / BOX
MESH = pl.DeviceIdType.MESH
F32 = jnp.float32
BF16 = jnp.bfloat16
VMEM_LIMIT = 56 * 1024 * 1024


def step_tables():
    k = np.arange(COEFS)
    kx = k % KX
    ky = k // KX - KY // 2
    cosine = np.zeros((16, COEFS), np.float32)
    sine = np.zeros((16, COEFS), np.float32)
    for a in range(TRANS):
        turn = (kx * (a // 3 - 1) + ky * (a % 3 - 1)) * RADIANS
        cosine[a] = np.cos(turn)
        sine[a] = np.sin(turn)
    return cosine, sine


def wrap(value, size):
    return lax.rem(value + size, size)


def nt_dot(left, right):
    return lax.dot_general(left, right, (((1,), (1,)), ((), ())), preferred_element_type=F32)


def tn_dot(left, right):
    return lax.dot_general(left, right, (((0,), (0,)), ((), ())), preferred_element_type=F32)


def slot_row(rows_ref, n):
    groups = []
    for q in range(4):
        parts = [rows_ref[4 * q + m, n:n + 1, :] for m in range(4)]
        groups.append((parts[0] + parts[1]) + (parts[2] + parts[3]))
    return jnp.concatenate(groups, axis=1)


def iota(shape, axis):
    return lax.broadcasted_iota(jnp.int32, shape, axis)


HALF = SLOTS // 2
COMBOS = 96
EARLY = 11
PIECE = HALF // 2


def wave_table():
    k = np.arange(COEFS)
    which = np.arange(COMBOS)[:, None]
    turn = ((k % KX) * (which // 9 - 4) + (k // KX - KY // 2) * (which % 9 - 4)) * RADIANS
    table = np.zeros((N_CLS, 2 * COMBOS, 2 * CHUNK), ml_dtypes.bfloat16)
    for n, wave in enumerate((np.cos(turn), np.sin(turn))):
        coarse = wave.astype(ml_dtypes.bfloat16)
        fine = (wave - coarse.astype(np.float64)).astype(ml_dtypes.bfloat16)
        for half, value in enumerate((coarse, fine)):
            cut = value.reshape(COMBOS, N_CLS, CHUNK).transpose(1, 0, 2)
            table[:, half * COMBOS:(half + 1) * COMBOS, n * CHUNK:(n + 1) * CHUNK] = cut
    return table


def expect_kernel(images_ref, proj_ref, wave_ref, ctf_ref, index_ref, centre_ref, ranges_ref, inv_ref, cos_ref, sin_ref,
                  yout_ref, w_ref, t_ref, cw_ref, log_ref,
                  ximg, pbuf, send, meta, metain, ys, pd, s_ref, joint, shared, maps, yc, hot, trig, buf_a, buf_b,
                  local_sem, z_send, z_recv, m_send, m_recv, f_send, p_send, g_recv, e_send, e_recv):
    c = lax.axis_index("cls")
    h = lax.axis_index("ori")
    x = lax.rem(c, SIDE)
    y = lax.div(c, SIDE)

    def at(dx, dy):
        return wrap(y + dy, SIDE) * SIDE + wrap(x + dx, SIDE)

    def rel(half, du, dv):
        if isinstance(half, int):
            return at(du, dv) if half == 0 else at(dv, du)
        return at(du + half * (dv - du), dv + half * (du - dv))

    barrier = pltpu.get_barrier_semaphore()

    def quad_peer(stage, j):
        if stage == 0:
            return at(j, 0), h
        if stage == 1:
            return at(0, j), h
        if stage == 2:
            return c, lax.div(h, 4) * 4 + lax.rem(h + j, 4)
        return c, lax.rem(h + 4 * j, N_ORI)

    def greet(step, carry):
        pl.semaphore_signal(barrier, inc=1, device_id=(c, wrap(h + step, N_ORI)), device_id_type=MESH)
        return carry

    for stage in (0, 1):
        for j in (1, 2, 3):
            pl.semaphore_signal(barrier, inc=1, device_id=quad_peer(stage, j), device_id_type=MESH)
    lax.fori_loop(1, N_ORI, greet, 0)
    lanes = pl.ds(pl.multiple_of(c * CHUNK, CHUNK), CHUNK)
    get_image = pltpu.make_async_copy(images_ref.at[:, :, lanes], ximg, local_sem.at[0])
    get_image.start()
    get_proj = pltpu.make_async_copy(proj_ref.at[0], pbuf, local_sem.at[1])
    get_proj.start()
    get_wave = pltpu.make_async_copy(
        wave_ref, trig.at[:, pl.ds(GROUPS, 2 * COMBOS), pl.ds(0, 2 * CHUNK)], local_sem.at[4]
    )
    get_wave.start()

    index_row = index_ref[...].astype(F32)
    member_t = jnp.zeros((N_ORI, PART), F32)
    rank = iota((N_ORI, PART), 0)
    for j in range(PRUNE):
        member_t = member_t + (ranges_ref[j:j + 1, :] == rank).astype(F32)
    above = (iota((PART, PART), 0) < iota((PART, PART), 1)).astype(BF16)
    before_t = jnp.dot(member_t.astype(BF16), above, preferred_element_type=F32)
    pos_t = before_t - 1000.0 * (1.0 - member_t)
    odd = lax.rem(h, 2).astype(F32)
    key = (before_t + 1.0) * member_t
    keys = jnp.concatenate([key * (1.0 - odd), key * odd], axis=1)
    seat = iota((CAP, PART), 0).astype(F32)
    chosen = jnp.concatenate(
        [(pos_t[r:r + 1, :] == seat).astype(BF16) for r in range(N_ORI)], axis=0
    )
    offset = (CAP * lax.rem(h, 4)).astype(F32)
    wide_seat = iota((128, PART), 0).astype(F32) - offset
    moves = centre_ref[...].astype(F32)
    combo = (moves[0:1, :] + 4.0) * 9.0 + moves[1:2, :] + 4.0
    label = jnp.concatenate([index_row + 1.0, combo, jnp.zeros((6, PART), F32)], axis=0).astype(BF16)
    for r in range(N_ORI):
        wide = (pos_t[r:r + 1, :] == wide_seat).astype(BF16)
        seated = nt_dot(label, wide)
        meta[r] = jnp.concatenate([seated[0:1, :], keys[r:r + 1, :], seated[1:3, :]], axis=0)
    get_image.wait()
    pixels = ximg[...].astype(F32)
    x0 = pixels[:, 0, :]
    x1 = pixels[:, 1, :]
    centred = jnp.concatenate([x0, x1], axis=1).astype(BF16)
    send[...] = jnp.dot(chosen, centred, preferred_element_type=F32).astype(BF16).reshape(N_ORI, CAP, 2 * CHUNK)

    pl.semaphore_wait(barrier, N_ORI - 1 + 6)

    def block_cols(block):
        return pl.ds(pl.multiple_of(block * 2 * CHUNK, 2 * CHUNK), 2 * CHUNK)

    def seat_rows(block):
        return pl.ds(pl.multiple_of(block * CAP, CAP), CAP)

    def parcel(peer, step):
        return pltpu.make_async_remote_copy(
            src_ref=send.at[peer], dst_ref=ys.at[seat_rows(h), block_cols(c)], send_sem=z_send.at[step],
            recv_sem=z_recv.at[h], device_id=(c, peer), device_id_type=MESH)

    def note(peer, step):
        return pltpu.make_async_remote_copy(
            src_ref=meta.at[peer], dst_ref=metain.at[h], send_sem=m_send.at[step],
            recv_sem=m_recv.at[h], device_id=(c, peer), device_id_type=MESH)

    def send_out(step, carry):
        peer = wrap(h + step, N_ORI)
        note(peer, step).start()
        parcel(peer, step).start()
        return carry

    lax.fori_loop(1, N_ORI, send_out, 0)
    own_rows = pltpu.make_async_copy(send.at[h], ys.at[seat_rows(h), block_cols(c)], local_sem.at[2])
    own_rows.start()
    metain[h] = meta[h]

    get_proj.wait()
    get_wave.wait()
    s_ref[0:ORI_DEV, 0:GROUPS] = jnp.zeros((ORI_DEV, GROUPS), F32)

    def turn_chunk(j, carry):
        cols = pl.ds(pl.multiple_of(j * CHUNK, CHUNK), CHUNK)
        both = pbuf[:, :, cols].astype(F32)
        p0 = both[:, 0, :]
        p1 = both[:, 1, :]
        power = (p0 * p0 + p1 * p1).astype(BF16)
        table = ctf_ref[:, cols].astype(F32)
        cw = (inv_ref[:, cols] * table * table).astype(BF16)
        cw_ref[:, cols] = cw
        s_ref[0:ORI_DEV, 0:GROUPS] += nt_dot(power, cw)
        for d in range(TRANS):
            rows = pl.ds(d * ORI_DEV, ORI_DEV)
            cd = cos_ref[d:d + 1, cols]
            sd = sin_ref[d:d + 1, cols]
            turned = (p0 * cd - p1 * sd, p1 * cd + p0 * sd)
            for n in (0, 1):
                coarse = turned[n].astype(BF16)
                pd[j, rows, n * CHUNK:(n + 1) * CHUNK] = coarse
                pd[j, rows, (2 + n) * CHUNK:(3 + n) * CHUNK] = (turned[n] - coarse.astype(F32)).astype(BF16)
        trig[j, 0:GROUPS, 0:2 * CHUNK] = jnp.zeros((GROUPS, 2 * CHUNK), BF16)
        trig[j, 0:GROUPS, 2 * CHUNK:3 * CHUNK] = ctf_ref[:, cols]
        trig[j, GROUPS:256, 2 * CHUNK:3 * CHUNK] = jnp.zeros((2 * COMBOS, CHUNK), BF16)
        return carry

    lax.fori_loop(0, EARLY, turn_chunk, 0)

    def arrive(step, carry):
        peer = wrap(h - step, N_ORI)
        pltpu.make_async_remote_copy(
            src_ref=send.at[h], dst_ref=ys.at[seat_rows(peer), block_cols(c)], send_sem=z_send.at[0],
            recv_sem=z_recv.at[peer], device_id=(c, peer), device_id_type=MESH).wait_recv()
        pltpu.make_async_remote_copy(
            src_ref=meta.at[h], dst_ref=metain.at[peer], send_sem=m_send.at[0],
            recv_sem=m_recv.at[peer], device_id=(c, peer), device_id_type=MESH).wait_recv()
        return carry

    own_rows.wait()
    lax.fori_loop(1, N_ORI, arrive, 0)

    def full_view(half, block):
        return ys.at[pl.ds(pl.multiple_of(half * HALF, HALF), HALF), block_cols(block)]

    def piece_view(half, block, piece):
        return ys.at[pl.ds(pl.multiple_of(half * HALF + piece * PIECE, PIECE), PIECE), block_cols(block)]

    def full_copy(half, block, target, slot):
        return pltpu.make_async_remote_copy(
            src_ref=full_view(half, block), dst_ref=full_view(half, block), send_sem=f_send.at[slot],
            recv_sem=g_recv.at[half, block, 0], device_id=(target, h), device_id_type=MESH)

    def piece_copy(half, block, piece, target, slot):
        return pltpu.make_async_remote_copy(
            src_ref=piece_view(half, block, piece), dst_ref=piece_view(half, block, piece),
            send_sem=p_send.at[slot], recv_sem=g_recv.at[half, block, piece],
            device_id=(target, h), device_id_type=MESH)

    def second_sends(half, du, t):
        for n, sign in enumerate((1, -1)):
            full_copy(half, rel(half, du, 0), rel(half, 0, sign), 4 + 4 * t + 2 * half + n).start()

    for half in (0, 1):
        for n, sign in enumerate((1, -1)):
            full_copy(half, rel(half, 0, 0), rel(half, sign, 0), 2 * half + n).start()
    for half in (0, 1):
        second_sends(half, 0, 0)

    lax.fori_loop(EARLY, N_CLS, turn_chunk, 0)
    row = slot_row(metain, 0) - 1.0
    slot_pick = (iota((GROUPS, SLOTS), 0).astype(F32) == row).astype(BF16)
    combo_pick = (iota((COMBOS, SLOTS), 0).astype(F32) == slot_row(metain, 2)).astype(BF16)
    eye = (iota((256, 256), 0) == iota((256, 256), 1)).astype(BF16)
    hot[...] = tn_dot(jnp.concatenate([slot_pick, combo_pick, combo_pick], axis=0), eye).astype(BF16)
    rest = s_ref[0:ORI_DEV, 0:GROUPS]
    energy = jnp.zeros((ORI_DEV, SLOTS), F32)
    for _ in range(3):
        part = rest.astype(BF16)
        rest = rest - part.astype(F32)
        energy = energy + jnp.dot(part, slot_pick, preferred_element_type=F32)
    less = -0.5 * energy - jnp.where(row < 0.0, 1e30, 0.0)
    for d in range(TRANS):
        s_ref[pl.ds(d * ORI_DEV, ORI_DEV), :] = less

    tall = iota((128, 128), 0).astype(F32)
    side = lax.div(iota((1, 128), 1), PART)
    listed = []
    for p in range(N_ORI // 2):
        keyed = metain[2 * p, 1:2, :] + metain[2 * p + 1, 1:2, :]
        listed.append(keyed)
        target = keyed - 1.0 + (CAP * (2 * (p % 2) + side)).astype(F32)
        target = jnp.where(keyed > 0.0, target, -1000.0)
        maps[p // 2, :, 128 * (p % 2):128 * (p % 2) + 128] = (tall == target).astype(BF16)

    def centre_rows(half, block, buf):
        rows = slice(half * HALF, half * HALF + HALF)
        freqs = pl.ds(pl.multiple_of(block * CHUNK, CHUNK), CHUNK)
        wave = jnp.dot(hot[rows, :], trig[block], preferred_element_type=F32)
        cs = wave[:, 0:CHUNK]
        sn = wave[:, CHUNK:2 * CHUNK]
        factor = wave[:, 2 * CHUNK:3 * CHUNK] * inv_ref[:, freqs]
        raw = ys[rows, block_cols(block)].astype(F32)
        x0 = raw[:, 0:CHUNK]
        x1 = raw[:, CHUNK:2 * CHUNK]
        value = jnp.concatenate([factor * (x0 * cs + x1 * sn), factor * (x1 * cs - x0 * sn)], axis=1)
        coarse = value.astype(BF16)
        buf[:, 0:2 * CHUNK] = coarse
        buf[:, 2 * CHUNK:4 * CHUNK] = (value - coarse.astype(F32)).astype(BF16)
        yc[rows, block_cols(block)] = coarse

    def add_scores(half, block, buf):
        first = pd[block, :, 0:2 * CHUNK]
        second = pd[block, :, 2 * CHUNK:4 * CHUNK]
        coarse = buf[:, 0:2 * CHUNK]
        fine = buf[:, 2 * CHUNK:4 * CHUNK]
        s_ref[:, half * HALF:half * HALF + HALF] += nt_dot(first, coarse) + (
            nt_dot(first, fine) + nt_dot(second, coarse)
        )

    def pair(before, du, dv):
        block = rel(0, du, dv)
        add_scores(1, before, buf_b)
        centre_rows(0, block, buf_a)
        block_b = rel(1, du, dv)
        add_scores(0, block, buf_a)
        centre_rows(1, block_b, buf_b)
        return block_b

    centre_rows(0, c, buf_a)
    add_scores(0, c, buf_a)
    centre_rows(1, c, buf_b)
    before = c
    for t, du, piece, onward in ((1, -1, 0, 1), (2, 1, 1, -1)):
        for half in (0, 1):
            full_copy(half, rel(half, du, 0), c, 0).wait_recv()
            piece_copy(half, rel(half, du, 0), piece, rel(half, onward, 0), 2 * half + piece).start()
        for half in (0, 1):
            second_sends(half, du, t)

    before = lax.fori_loop(0, 2, lambda n, block: pair(block, 2 * n - 1, 0), before)
    for half in (0, 1):
        for piece in (0, 1):
            piece_copy(half, rel(half, 2, 0), piece, c, 0).wait_recv()
        second_sends(half, 2, 3)

    before = pair(before, 2, 0)

    def gray(t):
        return t + lax.div(t, 2) * (1 - 2 * lax.rem(t, 2))

    def cross(t, carry):
        du = gray(t)
        for dv, piece, onward in ((-1, 0, 1), (1, 1, -1)):
            for half in (0, 1):
                full_copy(half, rel(half, du, dv), c, 0).wait_recv()
                piece_copy(half, rel(half, du, dv), piece, rel(half, 0, onward), 4 + 4 * t + 2 * half + piece).start()

        return lax.fori_loop(0, 2, lambda n, block: pair(block, du, 2 * n - 1), carry)

    before = lax.fori_loop(0, 4, cross, before)

    def corner(n, carry):
        du = gray(n)
        for half in (0, 1):
            for piece in (0, 1):
                piece_copy(half, rel(half, du, 2), piece, c, 0).wait_recv()
        return pair(carry, du, 2)

    before = lax.fori_loop(0, 4, corner, before)
    add_scores(1, before, buf_b)
    save = pltpu.make_async_copy(yc, yout_ref, local_sem.at[3])
    save.start()

    peak = s_ref[0:ORI_DEV, :]
    for d in range(1, TRANS):
        peak = jnp.maximum(peak, s_ref[pl.ds(d * ORI_DEV, ORI_DEV), :])
    peak = jnp.max(peak, axis=0, keepdims=True)
    mass = jnp.zeros((ORI_DEV, SLOTS), F32)
    for d in range(TRANS):
        rows = pl.ds(d * ORI_DEV, ORI_DEV)
        value = jnp.exp(s_ref[rows, :] - peak)
        s_ref[rows, :] = value
        mass = mass + value
    total = jnp.sum(mass, axis=0, keepdims=True)
    def split(value):
        parts = []
        for _ in range(3):
            part = value.astype(BF16).astype(F32)
            parts.append(part)
            value = value - part
        return parts

    blank = jnp.zeros((2, 128), F32)
    for q in range(4):
        span = slice(128 * q, 128 * q + 128)
        rows = jnp.concatenate(split(peak[:, span]) + split(total[:, span]) + [blank], axis=0).astype(BF16)
        spread = jnp.dot(rows, maps[q], preferred_element_type=F32)
        particle_peak = spread[0:1, :] + spread[1:2, :] + spread[2:3, :]
        particle_mass = spread[3:4, :] + spread[4:5, :] + spread[5:6, :]
        for n in (0, 1):
            half_span = slice(128 * n, 128 * n + 128)
            p = 2 * q + n
            joint[0, 0, p:p + 1, :] = jnp.where(listed[p] > 0.0, particle_peak[:, half_span], -3e38)
            joint[0, 1, p:p + 1, :] = particle_mass[:, half_span]

    def share(stage, j):
        return pltpu.make_async_remote_copy(
            src_ref=joint.at[stage], dst_ref=shared.at[stage, j - 1], send_sem=e_send.at[stage, j],
            recv_sem=e_recv.at[stage, j], device_id=quad_peer(stage, j), device_id_type=MESH)

    for stage in range(4):
        for j in (1, 2, 3):
            share(stage, j).start()
        for j in (1, 2, 3):
            share(stage, j).wait_recv()
        high = joint[stage, 0]
        for j in range(3):
            high = jnp.maximum(high, shared[stage, j, 0])
        heaps = [joint[stage, 1] * jnp.exp(joint[stage, 0] - high)]
        for j in range(3):
            heaps.append(shared[stage, j, 1] * jnp.exp(shared[stage, j, 0] - high))
        heap = (heaps[0] + heaps[2]) + (heaps[1] + heaps[3])
        if stage < 3:
            joint[stage + 1, 0] = high
            joint[stage + 1, 1] = heap
    log_all = high + jnp.log(heap)
    joint[4, 0] = log_all
    home_row = joint[4, 0, pl.ds(lax.div(h, 2), 1), :]
    log_ref[...] = jnp.where(lax.rem(h, 2) == 0, home_row[:, 0:PART], home_row[:, PART:2 * PART])
    groups = []
    for q in range(4):
        pair = jnp.concatenate([log_all[2 * q:2 * q + 1, :], log_all[2 * q + 1:2 * q + 2, :]], axis=1)
        rows = jnp.concatenate(split(pair) + [jnp.zeros((5, 256), F32)], axis=0).astype(BF16)
        back_row = nt_dot(rows, maps[q])
        groups.append(back_row[0:1, :] + back_row[1:2, :] + back_row[2:3, :])
    slot_log = jnp.concatenate(groups, axis=1)
    scale = float(N_CLS * PRUNE * ORI_DEV)
    level = jnp.where(row < 0.0, 0.0, scale * jnp.exp(peak - slot_log))
    for d in range(TRANS):
        rows = pl.ds(d * ORI_DEV, ORI_DEV)
        w_ref[rows, :] = (s_ref[rows, :] * level).astype(BF16)
    grouped = nt_dot((mass * level).astype(BF16), slot_pick)
    high = grouped.astype(BF16)
    t_ref[:, 0:GROUPS] = high
    t_ref[:, GROUPS:2 * GROUPS] = (grouped - high.astype(F32)).astype(BF16)

    def drain(step, carry):
        peer = wrap(h + step, N_ORI)
        parcel(peer, step).wait_send()
        note(peer, step).wait_send()
        return carry

    lax.fori_loop(1, N_ORI, drain, 0)

    def drain_blocks(slot, carry):
        full_copy(0, c, c, slot).wait_send()
        piece_copy(0, c, 0, c, slot).wait_send()
        return carry

    lax.fori_loop(0, 20, drain_blocks, 0)
    for stage in range(4):
        for j in (1, 2, 3):
            share(stage, j).wait_send()
    save.wait()


def expect(images, projections, waves, ctf_table, index_row, centre, ranges, inv_row, cosine, sine):
    vmem = pl.BlockSpec(memory_space=pltpu.VMEM)
    hbm = pl.BlockSpec(memory_space=pl.ANY)
    rows = TRANS * ORI_DEV
    dma = pltpu.SemaphoreType.DMA
    return pl.pallas_call(
        expect_kernel,
        out_shape=(
            jax.ShapeDtypeStruct((SLOTS, 2 * COEFS), BF16),
            jax.ShapeDtypeStruct((rows, SLOTS), BF16),
            jax.ShapeDtypeStruct((ORI_DEV, 2 * GROUPS), BF16),
            jax.ShapeDtypeStruct((GROUPS, COEFS), BF16),
            jax.ShapeDtypeStruct((1, PART), F32),
        ),
        in_specs=[hbm, hbm, hbm] + [vmem] * 7,
        out_specs=(hbm, vmem, vmem, vmem, vmem),
        scratch_shapes=[
            pltpu.VMEM((PART, 2, CHUNK), BF16),
            pltpu.VMEM((ORI_DEV, 2, COEFS), BF16),
            pltpu.VMEM((N_ORI, CAP, 2 * CHUNK), BF16),
            pltpu.VMEM((N_ORI, 4, 128), F32),
            pltpu.VMEM((N_ORI, 4, 128), F32),
            pltpu.VMEM((SLOTS, 2 * COEFS), BF16),
            pltpu.VMEM((N_CLS, rows, 4 * CHUNK), BF16),
            pltpu.VMEM((rows, SLOTS), F32),
            pltpu.VMEM((5, 2, N_ORI // 2, 128), F32),
            pltpu.VMEM((4, 3, 2, N_ORI // 2, 128), F32),
            pltpu.VMEM((4, 128, 256), BF16),
            pltpu.VMEM((SLOTS, 2 * COEFS), BF16),
            pltpu.VMEM((SLOTS, 256), BF16),
            pltpu.VMEM((N_CLS, 256, 3 * CHUNK), BF16),
            pltpu.VMEM((HALF, 4 * CHUNK), BF16),
            pltpu.VMEM((HALF, 4 * CHUNK), BF16),
            dma((5,)),
            dma((N_ORI,)),
            dma((N_ORI,)),
            dma((N_ORI,)),
            dma((N_ORI,)),
            dma((20,)),
            dma((20,)),
            dma((2, N_CLS, 2)),
            dma((4, 4)),
            dma((4, 4)),
        ],
        compiler_params=pltpu.CompilerParams(
            collective_id=0, has_side_effects=True, vmem_limit_bytes=VMEM_LIMIT
        ),
        name="expect",
    )(images, projections, waves, ctf_table, index_row, centre, ranges, inv_row, cosine, sine)


WIDE = 4


def back_kernel(w_ref, t_ref, y_ref, cw_ref, cos_ref, sin_ref, data_ref, ctf_ref, d_ref):
    cw = cw_ref[...]
    ctf_ref[0] = jnp.dot(t_ref[...], jnp.concatenate([cw, cw], axis=0), preferred_element_type=F32)
    d_ref[...] = jnp.dot(w_ref[...], y_ref[...], preferred_element_type=F32)

    def turn(minus, zero, plus, cd, sd):
        real = zero[0] + cd * (plus[0] + minus[0]) + sd * (plus[1] - minus[1])
        imag = zero[1] + cd * (plus[1] + minus[1]) - sd * (plus[0] - minus[0])
        return real, imag

    for part in range(WIDE):
        base = part * 2 * CHUNK
        cols = slice(part * CHUNK, part * CHUNK + CHUNK)
        for block in range(ORI_DEV // 16):
            outer = []
            for dx in range(3):
                inner = []
                for dy in range(3):
                    rows = pl.ds((dx * 3 + dy) * ORI_DEV + block * 16, 16)
                    inner.append((d_ref[rows, base:base + CHUNK], d_ref[rows, base + CHUNK:base + 2 * CHUNK]))
                outer.append(turn(*inner, cos_ref[5:6, cols], sin_ref[5:6, cols]))
            real, imag = turn(*outer, cos_ref[7:8, cols], sin_ref[7:8, cols])
            data_ref[0, block * 16:(block + 1) * 16, 0, cols] = real
            data_ref[0, block * 16:(block + 1) * 16, 1, cols] = imag


def back(w, t, ys, cw, cosine, sine):
    full = lambda *shape: pl.BlockSpec(shape, lambda j: (0,) * len(shape))
    return pl.pallas_call(
        back_kernel,
        out_shape=(
            jax.ShapeDtypeStruct((1, ORI_DEV, 2, COEFS), F32),
            jax.ShapeDtypeStruct((1, ORI_DEV, COEFS), F32),
        ),
        grid=(N_CLS // WIDE,),
        in_specs=[
            full(TRANS * ORI_DEV, SLOTS),
            full(ORI_DEV, 2 * GROUPS),
            pl.BlockSpec((SLOTS, WIDE * 2 * CHUNK), lambda j: (0, j)),
            pl.BlockSpec((GROUPS, WIDE * CHUNK), lambda j: (0, j)),
            pl.BlockSpec((16, WIDE * CHUNK), lambda j: (0, j)),
            pl.BlockSpec((16, WIDE * CHUNK), lambda j: (0, j)),
        ],
        out_specs=(
            pl.BlockSpec((1, ORI_DEV, 2, WIDE * CHUNK), lambda j: (0, 0, 0, j)),
            pl.BlockSpec((1, ORI_DEV, WIDE * CHUNK), lambda j: (0, 0, j)),
        ),
        scratch_shapes=[pltpu.VMEM((TRANS * ORI_DEV, WIDE * 2 * CHUNK), F32)],
        compiler_params=pltpu.CompilerParams(vmem_limit_bytes=VMEM_LIMIT),
        name="back",
    )(w, t, ys, cw, cosine, sine)


def shards(images, projections, ctf_table, ctf_index, centre, ranges, inv_noise):
    cosine, sine = (jnp.asarray(table) for table in step_tables())
    ys, w, t, cw, log_row = expect(
        images, projections, jnp.asarray(wave_table()), ctf_table, ctf_index.reshape(1, PART), centre.T, ranges.T,
        inv_noise.reshape(1, COEFS), cosine, sine,
    )
    data, ctf = back(w, t, ys, cw, cosine, sine)
    return data, ctf, log_row.reshape(PART)


def solution(mesh):
    placed = (
        P("ori", None, None),
        P("cls", "ori", None, None),
        P(),
        P("ori"),
        P("ori", None),
        P("ori", None),
        P(),
    )
    return jax.shard_map(
        shards,
        mesh=mesh,
        in_specs=placed,
        out_specs=(P("cls", "ori", None, None), P("cls", "ori", None), P("ori")),
        check_vma=False,
    )
```
